32 devices in a mesh: sub: 8 (over z, x), crs: 4 (over y, core).
Axes of the slice: x: 2, y: 2, z: 4, core: 2. Of those that a mesh axis runs over, the one named last changes fastest.
Arguments:
- schur_block: float32 [64, 1536, 1536], P('sub', 'crs'), as said below
- rigid_modes: float32 [64, 6, 1536], P('sub'), may hold values from -0.4375 to 0.4375
- coarse_inverse: float32 [384, 384], P('crs'), as said below
- dual_rhs: float32 [32, 64, 1536], P('crs', 'sub'), may hold values from -6 to 6
- stiff_diag: float32 [64, 1536], P('sub'), may hold values from 0.25 to 2.5
- face_length: int32 [64, 6], P('sub'), may hold values from 0 to 256, as said below
Outputs:
- multipliers: float32 [32, 64, 1536], P('crs', 'sub')
- projected: float32 [32, 64, 1536], P('crs', 'sub')
The draws below stay inside these ranges and needn't reach their ends.
Inputs may be any that keep to these rules, and one draw needn't show every extreme that they name: Equal on the two sides of a face: face_length[s, c] = face_length[partner(s, c), c]; 0 where partner(s, c) does not exist; at least 64 where it exists. Each schur_block[s] is symmetric positive definite. coarse_inverse is symmetric.
All inputs are finite; a program needn't handle non-finite values.
Results may differ from the reference program's by a relative error of at most 0.0003.
Values sent between devices are 32-bit elements; how exact they have to be, the bound alone decides.
A program may use at most 64 MiB of HBM per device.

```python
import math
import jax
import jax.numpy as jnp
import numpy as np
from jax import lax

NI = 1536
MODES = 6
LOADS = 32
ITERS = 2
SY = 2
SZ = 4
SUBS = 8
SLOT = 256
NSUB = 64
NC = 384


def schur_single(sub_key):
    first_key = jax.random.fold_in(sub_key, 1)
    second_key = jax.random.fold_in(sub_key, 2)
    raw = jax.random.normal(first_key, (NI, NI), jnp.float32)
    symmetric = (raw + raw.T) * (0.5 / math.sqrt(NI))
    diagonal = jax.random.uniform(second_key, (NI,), jnp.float32, 2.0, 3.5)
    rows_idx = lax.broadcasted_iota(jnp.int32, (NI, NI), 0)
    cols_idx = lax.broadcasted_iota(jnp.int32, (NI, NI), 1)
    return jnp.where(rows_idx == cols_idx, diagonal[:, None], symmetric)


def draw_schur_block(key, part):
    base_key = jax.random.fold_in(key, 11)
    return lax.map(lambda number: schur_single(jax.random.fold_in(base_key, number)), jnp.arange(NSUB, dtype=jnp.int32))


def draw_coarse_inverse(key, part):
    first_key = jax.random.fold_in(key, 21)
    second_key = jax.random.fold_in(key, 22)
    raw = jax.random.normal(first_key, (NC, NC), jnp.float32)
    symmetric = (raw + raw.T) * (0.1 / math.sqrt(NC))
    diagonal = jax.random.uniform(second_key, (NC,), jnp.float32, 0.4, 0.8)
    rows_idx = lax.broadcasted_iota(jnp.int32, (NC, NC), 0)
    cols_idx = lax.broadcasted_iota(jnp.int32, (NC, NC), 1)
    return jnp.where(rows_idx == cols_idx, diagonal[:, None], symmetric)


def draw_face_length(key, part):
    indices = jnp.arange(NSUB, dtype=jnp.int32)
    coords = [indices // SUBS, indices % SUBS // SZ, indices % SZ]
    extent = [NSUB // SUBS, SY, SZ]
    stride = [SUBS, SZ, 1]
    drawn = jax.random.randint(jax.random.fold_in(key, 31), (NSUB, 6), SLOT // 4, SLOT + 1, dtype=jnp.int32)
    drawn = drawn.at[0, 0].set(SLOT)
    columns = []
    for colour in range(6):
        axis_pick = colour // 2
        anchor = coords[axis_pick]
        offset = jnp.where(anchor % 2 == colour % 2, 1, -1)
        target = anchor + offset
        inside = (target >= 0) & (target < extent[axis_pick])
        lower = jnp.clip(jnp.minimum(indices, indices + offset * stride[axis_pick]), 0, NSUB - 1)
        columns.append(jnp.where(inside, drawn[lower, colour], 0))
    return jnp.stack(columns, axis=1).astype(jnp.int32)


def block_scale(rng, shape, shards, smallest, largest):
    def one(axis_at, shards_of):
        heights = jax.random.uniform(jax.random.fold_in(jax.random.fold_in(rng, 6), axis_at), (shards_of,), jnp.float32, smallest / len(shards), largest / len(shards))
        return jnp.repeat(jnp.exp(heights), shape[axis_at] // shards_of).reshape((-1,) + (1,) * (len(shape) - axis_at - 1))

    level = one(*shards[0])
    for cut in shards[1:]:
        level = level * one(*cut)
    return level


def normal_values(key, dims, spread, most, split=(), held_as=jnp.bfloat16):
    result = spread * jax.random.normal(key, dims, jnp.float32)
    if split:
        result = result * block_scale(key, dims, split, -0.22, 0.18)
    return jnp.clip(result, -most, most).astype(held_as)


def setup_inputs(seed: int = 0) -> dict:
    splits = jax.random.split(jax.random.key(seed), 7)
    return {
        "schur_block": draw_schur_block(jax.random.fold_in(splits[6], 71), 0),
        "rigid_modes": normal_values(splits[1], (NSUB, MODES, NI), (NI // 8) ** -0.5, 0.4375, ((0, 8),), jnp.float32),
        "coarse_inverse": draw_coarse_inverse(jax.random.fold_in(splits[6], 71), 0),
        "dual_rhs": normal_values(splits[3], (LOADS, NSUB, NI), 1.0, 6.0, ((0, 4), (1, 8)), jnp.float32),
        "stiff_diag": jnp.clip(jnp.exp(math.log(2.5) - 2.3025851 * jax.random.uniform(splits[4], (NSUB, NI), jnp.float32) ** block_scale(splits[4], (NSUB, NI), ((0, 8),), -0.2, 0.2)), 0.25, 2.5),
        "face_length": draw_face_length(jax.random.fold_in(splits[6], 71), 0),
    }


PRECISE = lax.Precision.HIGHEST


def partner_lookup():
    indices = np.arange(NSUB)
    coords = [indices // SUBS, (indices % SUBS) // SZ, indices % SZ]
    extent = [NSUB // SUBS, SY, SZ]
    stride = [SUBS, SZ, 1]
    lookup = np.zeros((6, NSUB), np.int32)
    for colour in range(6):
        axis_pick = colour // 2
        anchor = coords[axis_pick]
        offset = np.where(anchor % 2 == colour % 2, 1, -1)
        target = anchor + offset
        inside = (target >= 0) & (target < extent[axis_pick])
        lookup[colour] = np.where(inside, indices + offset * stride[axis_pick], indices)
    return lookup


def partner_values(vector, lookup):
    pieces = []
    for colour in range(6):
        window = vector[..., colour * SLOT:(colour + 1) * SLOT]
        pieces.append(jnp.take(window, jnp.asarray(lookup[colour]), axis=-2))
    return jnp.concatenate(pieces, axis=-1)


def inner(first_vec, second_vec):
    return 0.5 * jnp.sum(first_vec * second_vec, axis=(1, 2))


def reference(schur_block, rigid_modes, coarse_inverse, dual_rhs, stiff_diag, face_length):
    lookup = partner_lookup()
    positions = (jnp.arange(NI) % SLOT).astype(jnp.int32)
    usable = (jnp.repeat(face_length, SLOT, axis=1) > positions[None, :]).astype(jnp.float32)

    def assemble(vector):
        return usable * (vector - partner_values(vector, lookup))

    precond = usable * (stiff_diag + partner_values(stiff_diag, lookup))

    def project(vector):
        coarse = jnp.einsum('lsi,smi->lsm', vector, rigid_modes, precision=PRECISE).reshape(LOADS, NC)
        solved = jnp.einsum('lb,ab->la', coarse, coarse_inverse, precision=PRECISE).reshape(LOADS, NSUB, MODES)
        lifted = jnp.einsum('lsm,smi->lsi', solved, rigid_modes, precision=PRECISE)
        return vector - assemble(lifted)

    residual = assemble(dual_rhs)
    multipliers = jnp.zeros_like(residual)
    projected = project(residual)
    scaled = precond * projected
    energy = inner(projected, scaled)
    search = project(scaled)
    for iteration in range(ITERS):
        image = assemble(jnp.einsum('sij,lsj->lsi', schur_block, search, precision=PRECISE))
        step_size = energy / inner(search, image)
        multipliers = multipliers + step_size[:, None, None] * search
        residual = residual - step_size[:, None, None] * image
        projected = project(residual)
        if iteration + 1 < ITERS:
            scaled = precond * projected
            energy_new = inner(projected, scaled)
            search = project(scaled) + (energy_new / energy)[:, None, None] * search
            energy = energy_new
    return multipliers, projected
```

```python
import jax
import jax.numpy as jnp
import numpy as np
from jax import lax
from jax.sharding import PartitionSpec as P

ITERS = 2
SY = 2
SZ = 4
SUBS = 8

PRECISE = lax.Precision.HIGHEST
SPLIT = lax.Precision.HIGH


def local_lookup():
    indices = np.arange(SUBS)
    coords = [indices // SZ, indices % SZ]
    extent = [SY, SZ]
    stride = [SZ, 1]
    lookup = np.zeros((4, SUBS), np.int32)
    for colour in range(4):
        axis_pick = colour // 2
        anchor = coords[axis_pick]
        offset = np.where(anchor % 2 == colour % 2, 1, -1)
        target = anchor + offset
        inside = (target >= 0) & (target < extent[axis_pick])
        lookup[colour] = np.where(inside, indices + offset * stride[axis_pick], indices)
    return lookup


def shards(schur_block, rigid_modes, coarse_inverse, dual_rhs, stiff_diag, face_length):
    loads, subs, interface = dual_rhs.shape
    slot = interface // 6
    modes = rigid_modes.shape[1]
    own = subs * modes
    nsub = lax.axis_size("sub")
    sub_index = lax.axis_index("sub")
    even = sub_index % 2 == 0
    lookup = local_lookup()
    positions = jnp.arange(interface) % slot
    usable = (jnp.repeat(face_length, slot, axis=1) > positions[None, :]).astype(jnp.float32)
    up = [(i, i + 1) for i in range(nsub - 1)]
    down = [(i + 1, i) for i in range(nsub - 1)]

    def partner(vector):
        first = vector[..., :slot]
        second = vector[..., slot : 2 * slot]
        from_left = lax.ppermute(jnp.where(even, first, second), "sub", up)
        from_right = lax.ppermute(jnp.where(even, second, first), "sub", down)
        pieces = [jnp.where(even, from_right, from_left), jnp.where(even, from_left, from_right)]
        for colour in range(2, 6):
            window = vector[..., colour * slot : (colour + 1) * slot]
            pieces.append(
                jnp.concatenate([window[..., t : t + 1, :] for t in lookup[colour - 2]], axis=-2)
            )
        return jnp.concatenate(pieces, axis=-1)

    modes_first = jnp.swapaxes(rigid_modes, 0, 1)
    together = jnp.concatenate([dual_rhs, modes_first, stiff_diag[None]], axis=0)
    across = partner(together)
    residual = usable * (dual_rhs - across[:loads])
    modes_across = across[loads : loads + modes]
    precond = usable * (stiff_diag + across[-1])

    inverse = lax.all_gather(coarse_inverse, "crs", axis=0, tiled=True)

    def by_slot(array):
        return array.reshape(array.shape[:-1] + (6, slot))

    basis = by_slot(usable * jnp.concatenate([modes_first, -modes_across], axis=0))

    weighted = by_slot(modes_first * precond)
    blocks = jnp.einsum("msck,nsck->scmn", weighted, basis, precision=PRECISE)
    total_subs = nsub * subs
    here = sub_index * subs + jnp.arange(subs)
    left = here - subs
    right = here + subs
    targets = [jnp.where(even, right, left), jnp.where(even, left, right)]
    for colour in range(2, 6):
        targets.append(sub_index * subs + jnp.asarray(lookup[colour - 2]))
    targets = jnp.stack(targets, axis=1)
    hot_across = (targets[:, :, None] == jnp.arange(total_subs)).astype(jnp.float32)
    hot_here = (here[:, None] == jnp.arange(total_subs)).astype(jnp.float32)
    dense = jnp.einsum("smn,st->smtn", blocks[..., :modes].sum(axis=1), hot_here, precision=PRECISE)
    dense = dense + jnp.einsum("scmn,sct->smtn", blocks[..., modes:], hot_across, precision=PRECISE)
    dense = dense.reshape(own, total_subs * modes)
    middle = lax.all_gather(dense, "sub", axis=0, tiled=True)

    def coarse(vector):
        return jnp.einsum("lsi,msi->lsm", vector, modes_first, precision=PRECISE).reshape(loads, own)

    def dots(a, b):
        return jnp.sum(a * b, axis=(1, 2))[:, None]

    def shared(parts):
        gathered = lax.all_gather(jnp.concatenate(parts, axis=1), "sub", axis=0)
        count = own * (sum(part.shape[1] == own for part in parts))
        outs = []
        for at in range(0, count, own):
            outs.append(jnp.swapaxes(gathered[:, :, at : at + own], 0, 1).reshape(loads, nsub * own))
        sums = jnp.sum(gathered[:, :, count:], axis=0)
        return outs, [sums[:, j : j + 1] for j in range(sums.shape[1])]

    def solve(values):
        return jnp.einsum("lb,ab->la", values, inverse, precision=PRECISE)

    def lifted(values):
        grid = values.reshape(loads, nsub, subs, modes)
        padded = jnp.pad(grid, ((0, 0), (1, 1), (0, 0), (0, 0)))
        near = lax.dynamic_slice_in_dim(padded, sub_index, 3, axis=1)
        before, mine, after = near[:, 0], near[:, 1], near[:, 2]
        pieces = [jnp.where(even, after, before), jnp.where(even, before, after)]
        for colour in range(2, 6):
            pieces.append(jnp.stack([mine[:, t] for t in lookup[colour - 2]], axis=1))
        other = jnp.stack(pieces, axis=2)
        mine = jnp.broadcast_to(mine[:, :, None], other.shape)
        factors = jnp.concatenate([mine, other], axis=-1)
        out = jnp.einsum("lscm,msck->lsck", factors, basis, precision=PRECISE)
        return out.reshape(loads, subs, interface)

    def direction(residual, c_res, c_scaled, power):
        y = solve(c_res)
        my = jnp.einsum("lb,ab->la", y, middle, precision=PRECISE)
        energy = 0.5 * power - 2.0 * jnp.sum(y * c_scaled, axis=1, keepdims=True)
        energy = energy + jnp.sum(y * my, axis=1, keepdims=True)
        t = solve(c_scaled - my)
        return precond * (residual - lifted(y)) - lifted(t), energy

    scaled = precond * residual
    (c_res, c_scaled), (power,) = shared([coarse(residual), coarse(scaled), dots(residual, scaled)])
    search, energy = direction(residual, c_res, c_scaled, power)
    multipliers = None
    for iteration in range(ITERS):
        by_rows = jnp.einsum(
            "sij,lsj->lsi",
            schur_block,
            lax.all_gather(search, "crs", axis=0, tiled=True),
            precision=SPLIT,
        )
        product = lax.all_to_all(by_rows, "crs", split_axis=0, concat_axis=2, tiled=True)
        image = usable * (product - partner(product))
        last = iteration + 1 == ITERS
        curve = dots(search, product)
        if last:
            (c_image,), (curve,) = shared([coarse(image), curve])
        else:
            scaled_image = precond * image
            parts = [
                coarse(image),
                coarse(scaled_image),
                curve,
                dots(residual, scaled_image),
                dots(image, scaled_image),
            ]
            (c_image, c_scaled_image), (curve, cross, square) = shared(parts)
        step = energy / curve
        moved = step[:, :, None] * search
        multipliers = moved if multipliers is None else multipliers + moved
        residual = residual - step[:, :, None] * image
        c_res = c_res - step * c_image
        if last:
            projected = residual - lifted(solve(c_res))
        else:
            c_scaled = c_scaled - step * c_scaled_image
            power = power - 2.0 * step * cross + step * step * square
            fresh, energy_new = direction(residual, c_res, c_scaled, power)
            search = fresh + (energy_new / energy)[:, :, None] * search
            energy = energy_new
    return (multipliers, projected)


def solution(mesh):
    return jax.shard_map(
        shards,
        mesh=mesh,
        in_specs=(
            P("sub", "crs", None),
            P("sub", None, None),
            P("crs", None),
            P("crs", "sub", None),
            P("sub", None),
            P("sub", None),
        ),
        out_specs=(P("crs", "sub", None), P("crs", "sub", None)),
        check_vma=False,
    )
```

```python
import functools

import jax
import jax.numpy as jnp
import numpy as np
from jax import lax
from jax.experimental import pallas as pl
from jax.experimental.pallas import tpu as pltpu
from jax.sharding import PartitionSpec as P

ITERS = 2
SY = 2
SZ = 4
SUBS = 8

PRECISE = lax.Precision.HIGHEST
SPLIT = lax.Precision.HIGH


def local_lookup():
    indices = np.arange(SUBS)
    coords = [indices // SZ, indices % SZ]
    extent = [SY, SZ]
    stride = [SZ, 1]
    lookup = np.zeros((4, SUBS), np.int32)
    for colour in range(4):
        axis_pick = colour // 2
        anchor = coords[axis_pick]
        offset = np.where(anchor % 2 == colour % 2, 1, -1)
        target = anchor + offset
        inside = (target >= 0) & (target < extent[axis_pick])
        lookup[colour] = np.where(inside, indices + offset * stride[axis_pick], indices)
    return lookup


def by_collectives(schur_block, rigid_modes, coarse_inverse, dual_rhs, stiff_diag, face_length):
    loads, subs, interface = dual_rhs.shape
    slot = interface // 6
    modes = rigid_modes.shape[1]
    own = subs * modes
    nsub = lax.axis_size("sub")
    sub_index = lax.axis_index("sub")
    even = sub_index % 2 == 0
    lookup = local_lookup()
    positions = jnp.arange(interface) % slot
    usable = (jnp.repeat(face_length, slot, axis=1) > positions[None, :]).astype(jnp.float32)
    up = [(i, i + 1) for i in range(nsub - 1)]
    down = [(i + 1, i) for i in range(nsub - 1)]

    def partner(vector):
        first = vector[..., :slot]
        second = vector[..., slot : 2 * slot]
        from_left = lax.ppermute(jnp.where(even, first, second), "sub", up)
        from_right = lax.ppermute(jnp.where(even, second, first), "sub", down)
        pieces = [jnp.where(even, from_right, from_left), jnp.where(even, from_left, from_right)]
        for colour in range(2, 6):
            window = vector[..., colour * slot : (colour + 1) * slot]
            pieces.append(
                jnp.concatenate([window[..., t : t + 1, :] for t in lookup[colour - 2]], axis=-2)
            )
        return jnp.concatenate(pieces, axis=-1)

    modes_first = jnp.swapaxes(rigid_modes, 0, 1)
    together = jnp.concatenate([dual_rhs, modes_first, stiff_diag[None]], axis=0)
    across = partner(together)
    residual = usable * (dual_rhs - across[:loads])
    modes_across = across[loads : loads + modes]
    precond = usable * (stiff_diag + across[-1])

    inverse = lax.all_gather(coarse_inverse, "crs", axis=0, tiled=True)

    def by_slot(array):
        return array.reshape(array.shape[:-1] + (6, slot))

    basis = by_slot(usable * jnp.concatenate([modes_first, -modes_across], axis=0))

    weighted = by_slot(modes_first * precond)
    blocks = jnp.einsum("msck,nsck->scmn", weighted, basis, precision=PRECISE)
    total_subs = nsub * subs
    here = sub_index * subs + jnp.arange(subs)
    left = here - subs
    right = here + subs
    targets = [jnp.where(even, right, left), jnp.where(even, left, right)]
    for colour in range(2, 6):
        targets.append(sub_index * subs + jnp.asarray(lookup[colour - 2]))
    targets = jnp.stack(targets, axis=1)
    hot_across = (targets[:, :, None] == jnp.arange(total_subs)).astype(jnp.float32)
    hot_here = (here[:, None] == jnp.arange(total_subs)).astype(jnp.float32)
    dense = jnp.einsum("smn,st->smtn", blocks[..., :modes].sum(axis=1), hot_here, precision=PRECISE)
    dense = dense + jnp.einsum("scmn,sct->smtn", blocks[..., modes:], hot_across, precision=PRECISE)
    dense = dense.reshape(own, total_subs * modes)
    middle = lax.all_gather(dense, "sub", axis=0, tiled=True)

    def coarse(vector):
        return jnp.einsum("lsi,msi->lsm", vector, modes_first, precision=PRECISE).reshape(loads, own)

    def dots(a, b):
        return jnp.sum(a * b, axis=(1, 2))[:, None]

    def shared(parts):
        gathered = lax.all_gather(jnp.concatenate(parts, axis=1), "sub", axis=0)
        count = own * (sum(part.shape[1] == own for part in parts))
        outs = []
        for at in range(0, count, own):
            outs.append(jnp.swapaxes(gathered[:, :, at : at + own], 0, 1).reshape(loads, nsub * own))
        sums = jnp.sum(gathered[:, :, count:], axis=0)
        return outs, [sums[:, j : j + 1] for j in range(sums.shape[1])]

    def solve(values):
        return jnp.einsum("lb,ab->la", values, inverse, precision=PRECISE)

    def lifted(values):
        grid = values.reshape(loads, nsub, subs, modes)
        padded = jnp.pad(grid, ((0, 0), (1, 1), (0, 0), (0, 0)))
        near = lax.dynamic_slice_in_dim(padded, sub_index, 3, axis=1)
        before, mine, after = near[:, 0], near[:, 1], near[:, 2]
        pieces = [jnp.where(even, after, before), jnp.where(even, before, after)]
        for colour in range(2, 6):
            pieces.append(jnp.stack([mine[:, t] for t in lookup[colour - 2]], axis=1))
        other = jnp.stack(pieces, axis=2)
        mine = jnp.broadcast_to(mine[:, :, None], other.shape)
        factors = jnp.concatenate([mine, other], axis=-1)
        out = jnp.einsum("lscm,msck->lsck", factors, basis, precision=PRECISE)
        return out.reshape(loads, subs, interface)

    def direction(residual, c_res, c_scaled, power):
        y = solve(c_res)
        my = jnp.einsum("lb,ab->la", y, middle, precision=PRECISE)
        energy = 0.5 * power - 2.0 * jnp.sum(y * c_scaled, axis=1, keepdims=True)
        energy = energy + jnp.sum(y * my, axis=1, keepdims=True)
        t = solve(c_scaled - my)
        return precond * (residual - lifted(y)) - lifted(t), energy

    scaled = precond * residual
    (c_res, c_scaled), (power,) = shared([coarse(residual), coarse(scaled), dots(residual, scaled)])
    search, energy = direction(residual, c_res, c_scaled, power)
    multipliers = None
    for iteration in range(ITERS):
        by_rows = jnp.einsum(
            "sij,lsj->lsi",
            schur_block,
            lax.all_gather(search, "crs", axis=0, tiled=True),
            precision=SPLIT,
        )
        product = lax.all_to_all(by_rows, "crs", split_axis=0, concat_axis=2, tiled=True)
        image = usable * (product - partner(product))
        last = iteration + 1 == ITERS
        curve = dots(search, product)
        if last:
            (c_image,), (curve,) = shared([coarse(image), curve])
        else:
            scaled_image = precond * image
            parts = [
                coarse(image),
                coarse(scaled_image),
                curve,
                dots(residual, scaled_image),
                dots(image, scaled_image),
            ]
            (c_image, c_scaled_image), (curve, cross, square) = shared(parts)
        step = energy / curve
        moved = step[:, :, None] * search
        multipliers = moved if multipliers is None else multipliers + moved
        residual = residual - step[:, :, None] * image
        c_res = c_res - step * c_image
        if last:
            projected = residual - lifted(solve(c_res))
        else:
            c_scaled = c_scaled - step * c_scaled_image
            power = power - 2.0 * step * cross + step * step * square
            fresh, energy_new = direction(residual, c_res, c_scaled, power)
            search = fresh + (energy_new / energy)[:, :, None] * search
            energy = energy_new
    return (multipliers, projected)


MESH = pl.DeviceIdType.MESH


def across_rows(a, b, precision=None):
    return lax.dot_general(
        a, b, (((1,), (1,)), ((), ())), precision=precision, preferred_element_type=jnp.float32
    )


def halves(x):
    high = x.astype(jnp.bfloat16)
    return high, (x - high.astype(jnp.float32)).astype(jnp.bfloat16)


def operate_kernel(
    nsub,
    lookup,
    schur,
    search,
    usable,
    image,
    curve,
    hold,
    gath,
    res,
    product,
    across,
    load_sem,
    gsend,
    grecv,
    asend,
    arecv,
    osem,
    fsend,
    frecv,
):
    subs, loads, interface = search.shape
    rows = hold.shape[1]
    slot = interface // 6
    me = lax.axis_index("sub")
    q = lax.axis_index("crs")
    core = q % 2
    twin = q + 1 - 2 * core
    far = (q + 2) % 4
    diagonal = (twin + 2) % 4
    odd = me % 2
    first = me + 1 - 2 * odd
    second = me - 1 + 2 * odd
    has_second = jnp.logical_and(second >= 0, second < nsub)

    def load(s):
        return pltpu.make_async_copy(schur.at[s], hold.at[s], load_sem.at[s])

    def start_load(s, carry):
        load(s).start()
        return carry

    lax.fori_loop(0, subs, start_load, 0)
    barrier = pltpu.get_barrier_semaphore()
    for peer in (twin, far, diagonal):
        pl.semaphore_signal(barrier, inc=1, device_id=(me, peer), device_id_type=MESH)
    pl.semaphore_signal(barrier, inc=1, device_id=(first, q), device_id_type=MESH)

    @pl.when(has_second)
    def _():
        pl.semaphore_signal(barrier, inc=1, device_id=(second, q), device_id_type=MESH)

    pl.semaphore_wait(barrier, jnp.where(has_second, 5, 4))

    def remote(src, dst, send, recv, target):
        return pltpu.make_async_remote_copy(
            src_ref=src,
            dst_ref=dst,
            send_sem=send,
            recv_sem=recv,
            device_id=target,
            device_id_type=MESH,
        )

    def to_twin(s, block):
        return remote(search.at[s], gath.at[s, block], gsend.at[0, s], grecv.at[0, s], (me, twin))

    def to_far(s, block):
        return remote(search.at[s], gath.at[s, block], gsend.at[1, s], grecv.at[1, s], (me, far))

    def relay(s, source, block):
        return remote(
            gath.at[s, source], gath.at[s, block], gsend.at[2, s], grecv.at[2, s], (me, twin)
        )

    def spread(s, carry):
        to_far(s, q).start()
        to_twin(s, q).start()
        return carry

    lax.fori_loop(0, subs, spread, 0)
    gath[:, q] = search[...]

    def forward(s):
        to_far(s, far).wait_recv()
        relay(s, far, far).start()

    peers = (twin, far, diagonal)
    own_columns = pl.ds(pl.multiple_of(q * rows, 128), rows)

    def give(s, j):
        return remote(
            res.at[s, peers[j]],
            product.at[s, :, own_columns],
            asend.at[j, s],
            arecv.at[j, s],
            (me, peers[j]),
        )

    def taken(s, j):
        columns = pl.ds(pl.multiple_of(peers[j] * rows, 128), rows)
        return remote(
            res.at[s, peers[j]],
            product.at[s, :, columns],
            asend.at[j, s],
            arecv.at[j, s],
            (me, peers[j]),
        )

    def keep(s):
        return pltpu.make_async_copy(res.at[s, q], product.at[s, :, own_columns], osem.at[s])

    forward(0)

    def multiply(s, carry):
        @pl.when(s + 1 < subs)
        def _():
            forward(s + 1)

        load(s).wait()
        w_high, w_low = halves(hold[s])
        to_twin(s, twin).wait_recv()
        relay(s, far, diagonal).wait_recv()
        x_high, x_low = halves(gath[s].reshape(4 * loads, interface))
        both = across_rows(jnp.concatenate([x_high, x_low], axis=0), w_high)
        out = both[: 4 * loads] + both[4 * loads :] + across_rows(x_high, w_low)
        res[s] = out.reshape(4, loads, rows)
        for j in range(3):
            give(s, j).start()
        keep(s).start()
        return carry

    lax.fori_loop(0, subs, multiply, 0)

    def finish(s, carry):
        keep(s).wait()
        for j in range(3):
            taken(s, j).wait_recv()
        return carry

    lax.fori_loop(0, subs, finish, 0)

    def face(c, target):
        return remote(
            product.at[:, :, pl.ds(c * slot, slot)],
            across.at[c],
            fsend.at[c],
            frecv.at[c],
            (target, q),
        )

    face(0, first).start()

    @pl.when(has_second)
    def _():
        face(1, second).start()

    @pl.when(jnp.logical_not(has_second))
    def _():
        across[1] = jnp.zeros(across.shape[1:], jnp.float32)

    total = jnp.zeros((loads, interface), jnp.float32)
    for s in range(subs):
        total = total + search[s] * product[s]
        for c in range(2, 6):
            at = pl.ds(c * slot, slot)
            other = int(lookup[c - 2][s])
            image[s, :, at] = usable[s, :, at] * (product[s, :, at] - product[other, :, at])
    curve[...] = jnp.broadcast_to(jnp.sum(total, axis=1, keepdims=True), curve.shape)

    def drain(s, carry):
        to_twin(s, q).wait_send()
        to_far(s, q).wait_send()
        relay(s, far, far).wait_send()
        for j in range(3):
            give(s, j).wait_send()
        return carry

    lax.fori_loop(0, subs, drain, 0)
    face(0, first).wait()

    @pl.when(has_second)
    def _():
        face(1, second).wait()

    for c in range(2):
        at = pl.ds(c * slot, slot)
        for s in range(subs):
            image[s, :, at] = usable[s, :, at] * (product[s, :, at] - across[c, s])


def project_kernel(nsub, v, extra, modes, solver, basis, lifted, total, msg, gat, send, recv):
    subs, loads, _ = v.shape
    me = lax.axis_index("sub")
    q = lax.axis_index("crs")
    barrier = pltpu.get_barrier_semaphore()
    for k in range(1, nsub):
        pl.semaphore_signal(
            barrier, inc=1, device_id=((me + k) % nsub, q), device_id_type=MESH
        )
    msg[...] = extra[...]
    for s in range(subs):
        msg[:, 8 * s : 8 * s + 8] = across_rows(v[s], modes[s], PRECISE)
    pl.semaphore_wait(barrier, nsub - 1)

    def copy(k, block):
        return pltpu.make_async_remote_copy(
            src_ref=msg,
            dst_ref=gat.at[block],
            send_sem=send.at[k],
            recv_sem=recv.at[k],
            device_id=((me + k) % nsub, q),
            device_id_type=MESH,
        )

    for k in range(1, nsub):
        copy(k, me).start()
    gat[me] = msg[...]
    for k in range(1, nsub):
        copy(k, (me + nsub - k) % nsub).wait_recv()
    for k in range(1, nsub):
        copy(k, me).wait_send()
    pieces = [gat[t] for t in range(nsub)]
    total[...] = functools.reduce(lambda a, b: a + b, pieces)
    values = jnp.concatenate([piece[:, : 8 * subs] for piece in pieces], axis=1)
    y = across_rows(values, solver[...], PRECISE)
    for s in range(subs):
        lifted[s] = jnp.dot(
            y[:, 64 * s : 64 * s + 64],
            basis[s],
            precision=PRECISE,
            preferred_element_type=jnp.float32,
        )


def by_kernels(schur_block, rigid_modes, coarse_inverse, dual_rhs, stiff_diag, face_length):
    loads, subs, interface = dual_rhs.shape
    rows = schur_block.shape[1]
    slot = interface // 6
    modes = rigid_modes.shape[1]
    nsub = lax.axis_size("sub")
    sub_index = lax.axis_index("sub")
    even = sub_index % 2 == 0
    lookup = local_lookup()
    positions = jnp.arange(interface) % slot
    usable = (jnp.repeat(face_length, slot, axis=1) > positions[None, :]).astype(jnp.float32)
    up = [(i, i + 1) for i in range(nsub - 1)]
    down = [(i + 1, i) for i in range(nsub - 1)]
    f32 = jnp.float32

    def partner(vector):
        first = vector[..., :slot]
        second = vector[..., slot : 2 * slot]
        from_left = lax.ppermute(jnp.where(even, first, second), "sub", up)
        from_right = lax.ppermute(jnp.where(even, second, first), "sub", down)
        pieces = [jnp.where(even, from_right, from_left), jnp.where(even, from_left, from_right)]
        for colour in range(2, 6):
            window = vector[..., colour * slot : (colour + 1) * slot]
            pieces.append(
                jnp.concatenate([window[t : t + 1] for t in lookup[colour - 2]], axis=0)
            )
        return jnp.concatenate(pieces, axis=-1)

    rhs = jnp.swapaxes(dual_rhs, 0, 1)
    wide = jnp.pad(rigid_modes, ((0, 0), (0, 8 - modes), (0, 0)))
    marked = jnp.concatenate([wide[:, :modes], stiff_diag[:, None], wide[:, modes + 1 :]], axis=1)
    together = jnp.concatenate([rhs, marked], axis=1)
    across = partner(together)
    mask = usable[:, None, :]
    residual = mask * (rhs - across[:, :loads])
    precond = mask * (stiff_diag[:, None] + across[:, loads + modes : loads + modes + 1])

    inverse = lax.all_gather(coarse_inverse, "crs", axis=0, tiled=True)
    count = nsub * subs
    table = jnp.pad(
        inverse.reshape(nsub, subs, modes, count, modes),
        ((1, 1), (0, 0), (0, 8 - modes), (0, 0), (0, 8 - modes)),
    ).reshape(nsub + 2, subs, 8, count * 8)
    near = lax.dynamic_slice_in_dim(table, sub_index, 3, axis=0)
    before, mine, after = near[0], near[1], near[2]
    picks = [mine, jnp.where(even, after, before), jnp.where(even, before, after)]
    for colour in range(2, 6):
        picks.append(jnp.stack([mine[t] for t in lookup[colour - 2]]))
    picks.append(jnp.zeros_like(mine))
    solver = jnp.stack(picks, axis=1).reshape(subs * 64, count * 8)

    other = jnp.pad(-mask * across[:, loads : loads + modes], ((0, 0), (0, 8 - modes), (0, 0)))
    slots = jnp.asarray(np.repeat(np.eye(6, dtype=np.float32), slot, axis=1))
    spread = (other[:, None] * slots[None, :, None, :]).reshape(subs, 48, interface)
    basis = jnp.concatenate([wide * mask, spread, jnp.zeros((subs, 8, interface), f32)], axis=1)

    vector = jax.ShapeDtypeStruct((subs, loads, interface), f32)
    small = jax.ShapeDtypeStruct((loads, 128), f32)
    vmem = pl.BlockSpec(memory_space=pltpu.VMEM)
    anywhere = pl.BlockSpec(memory_space=pl.ANY)
    dma = pltpu.SemaphoreType.DMA

    def operate(search):
        return pl.pallas_call(
            functools.partial(operate_kernel, nsub, lookup),
            out_shape=(vector, small),
            in_specs=[anywhere, vmem, vmem],
            out_specs=(vmem, vmem),
            scratch_shapes=[
                pltpu.VMEM((subs, rows, interface), f32),
                pltpu.VMEM((subs, 4, loads, interface), f32),
                pltpu.VMEM((subs, 4, loads, rows), f32),
                pltpu.VMEM((subs, loads, interface), f32),
                pltpu.VMEM((2, subs, loads, slot), f32),
                dma((subs,)),
                dma((3, subs)),
                dma((3, subs)),
                dma((3, subs)),
                dma((3, subs)),
                dma((subs,)),
                dma((2,)),
                dma((2,)),
            ],
            compiler_params=pltpu.CompilerParams(
                collective_id=0, has_side_effects=True, vmem_limit_bytes=48 * 1024 * 1024
            ),
            name="operate",
        )(schur_block, search, mask)

    def lift(v, extra):
        out, total = pl.pallas_call(
            functools.partial(project_kernel, nsub),
            out_shape=(vector, small),
            in_specs=[vmem] * 5,
            out_specs=(vmem, vmem),
            scratch_shapes=[
                pltpu.VMEM((loads, 128), f32),
                pltpu.VMEM((nsub, loads, 128), f32),
                dma((nsub,)),
                dma((nsub,)),
            ],
            compiler_params=pltpu.CompilerParams(
                collective_id=1, has_side_effects=True, vmem_limit_bytes=32 * 1024 * 1024
            ),
            name="lift",
        )(v, extra, wide, solver, basis)
        return out, total[:, 64:65]

    def dots(a, b):
        return jnp.broadcast_to(jnp.sum(a * b, axis=(0, 2))[:, None], (loads, 128))

    lifted, _ = lift(residual, jnp.zeros((loads, 128), f32))
    projected = residual - lifted
    scaled = precond * projected
    lifted, energy = lift(scaled, 0.5 * dots(projected, scaled))
    search = scaled - lifted
    multipliers = None
    for iteration in range(ITERS):
        image, curve = operate(search)
        lifted, curve = lift(image, curve)
        step = energy / curve
        moved = step[None] * search
        multipliers = moved if multipliers is None else multipliers + moved
        projected = projected - step[None] * (image - lifted)
        if iteration + 1 < ITERS:
            scaled = precond * projected
            lifted, energy_new = lift(scaled, 0.5 * dots(projected, scaled))
            search = scaled - lifted + (energy_new / energy)[None] * search
            energy = energy_new
    return (jnp.swapaxes(multipliers, 0, 1), jnp.swapaxes(projected, 0, 1))


def shards(schur_block, rigid_modes, coarse_inverse, dual_rhs, stiff_diag, face_length):
    fits = dual_rhs.shape[0] == 8 and lax.axis_size("crs") == 4 and lax.axis_size("sub") <= 8
    build = by_kernels if fits else by_collectives
    return build(schur_block, rigid_modes, coarse_inverse, dual_rhs, stiff_diag, face_length)


def solution(mesh):
    return jax.shard_map(
        shards,
        mesh=mesh,
        in_specs=(
            P("sub", "crs", None),
            P("sub", None, None),
            P("crs", None),
            P("crs", "sub", None),
            P("sub", None),
            P("sub", None),
        ),
        out_specs=(P("crs", "sub", None), P("crs", "sub", None)),
        check_vma=False,
    )
```

```python
import functools

import jax
import jax.numpy as jnp
import numpy as np
from jax import lax
from jax.experimental import pallas as pl
from jax.experimental.pallas import tpu as pltpu
from jax.sharding import PartitionSpec as P

ITERS = 2
SY = 2
SZ = 4
SUBS = 8

PRECISE = lax.Precision.HIGHEST
SPLIT = lax.Precision.HIGH


def local_lookup():
    indices = np.arange(SUBS)
    coords = [indices // SZ, indices % SZ]
    extent = [SY, SZ]
    stride = [SZ, 1]
    lookup = np.zeros((4, SUBS), np.int32)
    for colour in range(4):
        axis_pick = colour // 2
        anchor = coords[axis_pick]
        offset = np.where(anchor % 2 == colour % 2, 1, -1)
        target = anchor + offset
        inside = (target >= 0) & (target < extent[axis_pick])
        lookup[colour] = np.where(inside, indices + offset * stride[axis_pick], indices)
    return lookup


def by_collectives(schur_block, rigid_modes, coarse_inverse, dual_rhs, stiff_diag, face_length):
    loads, subs, interface = dual_rhs.shape
    slot = interface // 6
    modes = rigid_modes.shape[1]
    own = subs * modes
    nsub = lax.axis_size("sub")
    sub_index = lax.axis_index("sub")
    even = sub_index % 2 == 0
    lookup = local_lookup()
    positions = jnp.arange(interface) % slot
    usable = (jnp.repeat(face_length, slot, axis=1) > positions[None, :]).astype(jnp.float32)
    up = [(i, i + 1) for i in range(nsub - 1)]
    down = [(i + 1, i) for i in range(nsub - 1)]

    def partner(vector):
        first = vector[..., :slot]
        second = vector[..., slot : 2 * slot]
        from_left = lax.ppermute(jnp.where(even, first, second), "sub", up)
        from_right = lax.ppermute(jnp.where(even, second, first), "sub", down)
        pieces = [jnp.where(even, from_right, from_left), jnp.where(even, from_left, from_right)]
        for colour in range(2, 6):
            window = vector[..., colour * slot : (colour + 1) * slot]
            pieces.append(
                jnp.concatenate([window[..., t : t + 1, :] for t in lookup[colour - 2]], axis=-2)
            )
        return jnp.concatenate(pieces, axis=-1)

    modes_first = jnp.swapaxes(rigid_modes, 0, 1)
    together = jnp.concatenate([dual_rhs, modes_first, stiff_diag[None]], axis=0)
    across = partner(together)
    residual = usable * (dual_rhs - across[:loads])
    modes_across = across[loads : loads + modes]
    precond = usable * (stiff_diag + across[-1])

    inverse = lax.all_gather(coarse_inverse, "crs", axis=0, tiled=True)

    def by_slot(array):
        return array.reshape(array.shape[:-1] + (6, slot))

    basis = by_slot(usable * jnp.concatenate([modes_first, -modes_across], axis=0))

    weighted = by_slot(modes_first * precond)
    blocks = jnp.einsum("msck,nsck->scmn", weighted, basis, precision=PRECISE)
    total_subs = nsub * subs
    here = sub_index * subs + jnp.arange(subs)
    left = here - subs
    right = here + subs
    targets = [jnp.where(even, right, left), jnp.where(even, left, right)]
    for colour in range(2, 6):
        targets.append(sub_index * subs + jnp.asarray(lookup[colour - 2]))
    targets = jnp.stack(targets, axis=1)
    hot_across = (targets[:, :, None] == jnp.arange(total_subs)).astype(jnp.float32)
    hot_here = (here[:, None] == jnp.arange(total_subs)).astype(jnp.float32)
    dense = jnp.einsum("smn,st->smtn", blocks[..., :modes].sum(axis=1), hot_here, precision=PRECISE)
    dense = dense + jnp.einsum("scmn,sct->smtn", blocks[..., modes:], hot_across, precision=PRECISE)
    dense = dense.reshape(own, total_subs * modes)
    middle = lax.all_gather(dense, "sub", axis=0, tiled=True)

    def coarse(vector):
        return jnp.einsum("lsi,msi->lsm", vector, modes_first, precision=PRECISE).reshape(loads, own)

    def dots(a, b):
        return jnp.sum(a * b, axis=(1, 2))[:, None]

    def shared(parts):
        gathered = lax.all_gather(jnp.concatenate(parts, axis=1), "sub", axis=0)
        count = own * (sum(part.shape[1] == own for part in parts))
        outs = []
        for at in range(0, count, own):
            outs.append(jnp.swapaxes(gathered[:, :, at : at + own], 0, 1).reshape(loads, nsub * own))
        sums = jnp.sum(gathered[:, :, count:], axis=0)
        return outs, [sums[:, j : j + 1] for j in range(sums.shape[1])]

    def solve(values):
        return jnp.einsum("lb,ab->la", values, inverse, precision=PRECISE)

    def lifted(values):
        grid = values.reshape(loads, nsub, subs, modes)
        padded = jnp.pad(grid, ((0, 0), (1, 1), (0, 0), (0, 0)))
        near = lax.dynamic_slice_in_dim(padded, sub_index, 3, axis=1)
        before, mine, after = near[:, 0], near[:, 1], near[:, 2]
        pieces = [jnp.where(even, after, before), jnp.where(even, before, after)]
        for colour in range(2, 6):
            pieces.append(jnp.stack([mine[:, t] for t in lookup[colour - 2]], axis=1))
        other = jnp.stack(pieces, axis=2)
        mine = jnp.broadcast_to(mine[:, :, None], other.shape)
        factors = jnp.concatenate([mine, other], axis=-1)
        out = jnp.einsum("lscm,msck->lsck", factors, basis, precision=PRECISE)
        return out.reshape(loads, subs, interface)

    def direction(residual, c_res, c_scaled, power):
        y = solve(c_res)
        my = jnp.einsum("lb,ab->la", y, middle, precision=PRECISE)
        energy = 0.5 * power - 2.0 * jnp.sum(y * c_scaled, axis=1, keepdims=True)
        energy = energy + jnp.sum(y * my, axis=1, keepdims=True)
        t = solve(c_scaled - my)
        return precond * (residual - lifted(y)) - lifted(t), energy

    scaled = precond * residual
    (c_res, c_scaled), (power,) = shared([coarse(residual), coarse(scaled), dots(residual, scaled)])
    search, energy = direction(residual, c_res, c_scaled, power)
    multipliers = None
    for iteration in range(ITERS):
        by_rows = jnp.einsum(
            "sij,lsj->lsi",
            schur_block,
            lax.all_gather(search, "crs", axis=0, tiled=True),
            precision=SPLIT,
        )
        product = lax.all_to_all(by_rows, "crs", split_axis=0, concat_axis=2, tiled=True)
        image = usable * (product - partner(product))
        last = iteration + 1 == ITERS
        curve = dots(search, product)
        if last:
            (c_image,), (curve,) = shared([coarse(image), curve])
        else:
            scaled_image = precond * image
            parts = [
                coarse(image),
                coarse(scaled_image),
                curve,
                dots(residual, scaled_image),
                dots(image, scaled_image),
            ]
            (c_image, c_scaled_image), (curve, cross, square) = shared(parts)
        step = energy / curve
        moved = step[:, :, None] * search
        multipliers = moved if multipliers is None else multipliers + moved
        residual = residual - step[:, :, None] * image
        c_res = c_res - step * c_image
        if last:
            projected = residual - lifted(solve(c_res))
        else:
            c_scaled = c_scaled - step * c_scaled_image
            power = power - 2.0 * step * cross + step * step * square
            fresh, energy_new = direction(residual, c_res, c_scaled, power)
            search = fresh + (energy_new / energy)[:, :, None] * search
            energy = energy_new
    return (multipliers, projected)


MESH = pl.DeviceIdType.MESH


def across_rows(a, b, precision=None):
    return lax.dot_general(
        a, b, (((1,), (1,)), ((), ())), precision=precision, preferred_element_type=jnp.float32
    )


def halves(x):
    high = x.astype(jnp.bfloat16)
    return high, (x - high.astype(jnp.float32)).astype(jnp.bfloat16)


def operate_kernel(
    nsub,
    lookup,
    schur,
    search,
    usable,
    image,
    curve,
    hold,
    gath,
    res,
    product,
    across,
    load_sem,
    gsend,
    grecv,
    asend,
    arecv,
    osem,
    fsend,
    frecv,
):
    subs, loads, interface = search.shape
    rows = hold.shape[1]
    slot = interface // 6
    me = lax.axis_index("sub")
    q = lax.axis_index("crs")
    core = q % 2
    twin = q + 1 - 2 * core
    far = (q + 2) % 4
    diagonal = (twin + 2) % 4
    odd = me % 2
    first = me + 1 - 2 * odd
    second = me - 1 + 2 * odd
    has_second = jnp.logical_and(second >= 0, second < nsub)

    def load(s):
        return pltpu.make_async_copy(schur.at[s], hold.at[s], load_sem.at[s])

    def start_load(s, carry):
        load(s).start()
        return carry

    lax.fori_loop(0, subs, start_load, 0)
    barrier = pltpu.get_barrier_semaphore()
    for peer in (twin, far, diagonal):
        pl.semaphore_signal(barrier, inc=1, device_id=(me, peer), device_id_type=MESH)
    pl.semaphore_signal(barrier, inc=1, device_id=(first, q), device_id_type=MESH)

    @pl.when(has_second)
    def _():
        pl.semaphore_signal(barrier, inc=1, device_id=(second, q), device_id_type=MESH)

    pl.semaphore_wait(barrier, jnp.where(has_second, 5, 4))

    def remote(src, dst, send, recv, target):
        return pltpu.make_async_remote_copy(
            src_ref=src,
            dst_ref=dst,
            send_sem=send,
            recv_sem=recv,
            device_id=target,
            device_id_type=MESH,
        )

    def to_twin(s, block):
        return remote(search.at[s], gath.at[s, block], gsend.at[0, s], grecv.at[0, s], (me, twin))

    def to_far(s, block):
        return remote(search.at[s], gath.at[s, block], gsend.at[1, s], grecv.at[1, s], (me, far))

    def relay(s, source, block):
        return remote(
            gath.at[s, source], gath.at[s, block], gsend.at[2, s], grecv.at[2, s], (me, twin)
        )

    def spread(s, carry):
        to_far(s, q).start()
        to_twin(s, q).start()
        return carry

    lax.fori_loop(0, subs, spread, 0)
    gath[:, q] = search[...]

    def forward(s):
        to_far(s, far).wait_recv()
        relay(s, far, far).start()

    peers = (twin, far, diagonal)
    own_columns = pl.ds(pl.multiple_of(q * rows, 128), rows)

    def give(s, j):
        return remote(
            res.at[s, peers[j]],
            product.at[s, :, own_columns],
            asend.at[j, s],
            arecv.at[j, s],
            (me, peers[j]),
        )

    def taken(s, j):
        columns = pl.ds(pl.multiple_of(peers[j] * rows, 128), rows)
        return remote(
            res.at[s, peers[j]],
            product.at[s, :, columns],
            asend.at[j, s],
            arecv.at[j, s],
            (me, peers[j]),
        )

    def keep(s):
        return pltpu.make_async_copy(res.at[s, q], product.at[s, :, own_columns], osem.at[s])

    forward(0)

    def multiply(s, carry):
        @pl.when(s + 1 < subs)
        def _():
            forward(s + 1)

        load(s).wait()
        w_high, w_low = halves(hold[s])
        to_twin(s, twin).wait_recv()
        relay(s, far, diagonal).wait_recv()
        x_high, x_low = halves(gath[s].reshape(4 * loads, interface))
        both = across_rows(jnp.concatenate([x_high, x_low], axis=0), w_high)
        out = both[: 4 * loads] + both[4 * loads :] + across_rows(x_high, w_low)
        res[s] = out.reshape(4, loads, rows)
        for j in range(3):
            give(s, j).start()
        keep(s).start()
        return carry

    lax.fori_loop(0, subs, multiply, 0)

    def finish(s, carry):
        keep(s).wait()
        for j in range(3):
            taken(s, j).wait_recv()
        return carry

    lax.fori_loop(0, subs, finish, 0)

    def face(c, target):
        return remote(
            product.at[:, :, pl.ds(c * slot, slot)],
            across.at[c],
            fsend.at[c],
            frecv.at[c],
            (target, q),
        )

    face(0, first).start()

    @pl.when(has_second)
    def _():
        face(1, second).start()

    @pl.when(jnp.logical_not(has_second))
    def _():
        across[1] = jnp.zeros(across.shape[1:], jnp.float32)

    total = jnp.zeros((loads, interface), jnp.float32)
    for s in range(subs):
        total = total + search[s] * product[s]
        for c in range(2, 6):
            at = pl.ds(c * slot, slot)
            other = int(lookup[c - 2][s])
            image[s, :, at] = usable[s, :, at] * (product[s, :, at] - product[other, :, at])
    curve[...] = jnp.broadcast_to(jnp.sum(total, axis=1, keepdims=True), curve.shape)

    def drain(s, carry):
        to_twin(s, q).wait_send()
        to_far(s, q).wait_send()
        relay(s, far, far).wait_send()
        for j in range(3):
            give(s, j).wait_send()
        return carry

    lax.fori_loop(0, subs, drain, 0)
    face(0, first).wait()

    @pl.when(has_second)
    def _():
        face(1, second).wait()

    for c in range(2):
        at = pl.ds(c * slot, slot)
        for s in range(subs):
            image[s, :, at] = usable[s, :, at] * (product[s, :, at] - across[c, s])


def project_kernel(nsub, v, extra, modes, solver, basis, lifted, total, msg, gat, send, recv):
    subs, loads, _ = v.shape
    me = lax.axis_index("sub")
    q = lax.axis_index("crs")
    barrier = pltpu.get_barrier_semaphore()
    for k in range(1, nsub):
        pl.semaphore_signal(
            barrier, inc=1, device_id=((me + k) % nsub, q), device_id_type=MESH
        )
    msg[...] = extra[...]
    for s in range(subs):
        msg[:, 8 * s : 8 * s + 8] = across_rows(v[s], modes[s], PRECISE)
    pl.semaphore_wait(barrier, nsub - 1)

    def copy(k, block):
        return pltpu.make_async_remote_copy(
            src_ref=msg,
            dst_ref=gat.at[block],
            send_sem=send.at[k],
            recv_sem=recv.at[k],
            device_id=((me + k) % nsub, q),
            device_id_type=MESH,
        )

    for k in range(1, nsub):
        copy(k, me).start()
    gat[me] = msg[...]
    for k in range(1, nsub):
        copy(k, (me + nsub - k) % nsub).wait_recv()
    for k in range(1, nsub):
        copy(k, me).wait_send()
    pieces = [gat[t] for t in range(nsub)]
    total[...] = functools.reduce(lambda a, b: a + b, pieces)
    values = jnp.concatenate([piece[:, : 8 * subs] for piece in pieces], axis=1)
    y = across_rows(values, solver[...], PRECISE)
    for s in range(subs):
        lifted[s] = jnp.dot(
            y[:, 64 * s : 64 * s + 64],
            basis[s],
            precision=PRECISE,
            preferred_element_type=jnp.float32,
        )


def begin_kernel(nsub, edges, block, across, inverse, fsend, frecv, gsend, grecv, osem):
    me = lax.axis_index("sub")
    q = lax.axis_index("crs")
    core = q % 2
    twin = q + 1 - 2 * core
    far = (q + 2) % 4
    diagonal = (twin + 2) % 4
    odd = me % 2
    first = me + 1 - 2 * odd
    second = me - 1 + 2 * odd
    has_second = jnp.logical_and(second >= 0, second < nsub)
    slot = across.shape[3]
    barrier = pltpu.get_barrier_semaphore()
    for peer in (twin, far):
        pl.semaphore_signal(barrier, inc=1, device_id=(me, peer), device_id_type=MESH)
    pl.semaphore_signal(barrier, inc=1, device_id=(first, q), device_id_type=MESH)

    @pl.when(has_second)
    def _():
        pl.semaphore_signal(barrier, inc=1, device_id=(second, q), device_id_type=MESH)

    pl.semaphore_wait(barrier, jnp.where(has_second, 4, 3))

    def remote(src, dst, send, recv, target):
        return pltpu.make_async_remote_copy(
            src_ref=src,
            dst_ref=dst,
            send_sem=send,
            recv_sem=recv,
            device_id=target,
            device_id_type=MESH,
        )

    def to_far(at):
        return remote(block, inverse.at[at], gsend.at[1], grecv.at[1], (me, far))

    def to_twin(at):
        return remote(block, inverse.at[at], gsend.at[0], grecv.at[0], (me, twin))

    def relay(at):
        return remote(inverse.at[far], inverse.at[at], gsend.at[2], grecv.at[2], (me, twin))

    def face(c, target):
        return remote(
            edges.at[:, :, pl.ds(c * slot, slot)],
            across.at[c],
            fsend.at[c],
            frecv.at[c],
            (target, q),
        )

    keep = pltpu.make_async_copy(block, inverse.at[q], osem)
    to_far(q).start()
    to_twin(q).start()
    face(0, first).start()

    @pl.when(has_second)
    def _():
        face(1, second).start()

    keep.start()

    @pl.when(jnp.logical_not(has_second))
    def _():
        across[1] = jnp.zeros(across.shape[1:], jnp.float32)

    to_far(far).wait_recv()
    relay(far).start()
    keep.wait()
    to_twin(twin).wait_recv()
    to_far(q).wait_send()
    to_twin(q).wait_send()
    face(0, first).wait()

    @pl.when(has_second)
    def _():
        face(1, second).wait()

    relay(diagonal).wait_recv()
    relay(far).wait_send()


def by_kernels(schur_block, rigid_modes, coarse_inverse, dual_rhs, stiff_diag, face_length):
    loads, subs, interface = dual_rhs.shape
    rows = schur_block.shape[1]
    slot = interface // 6
    modes = rigid_modes.shape[1]
    nsub = lax.axis_size("sub")
    sub_index = lax.axis_index("sub")
    even = sub_index % 2 == 0
    lookup = local_lookup()
    positions = jnp.arange(interface) % slot
    usable = (jnp.repeat(face_length, slot, axis=1) > positions[None, :]).astype(jnp.float32)
    f32 = jnp.float32

    vmem = pl.BlockSpec(memory_space=pltpu.VMEM)
    anywhere = pl.BlockSpec(memory_space=pl.ANY)
    dma = pltpu.SemaphoreType.DMA

    rhs = jnp.swapaxes(dual_rhs, 0, 1)
    wide = jnp.pad(rigid_modes, ((0, 0), (0, 8 - modes), (0, 0)))
    marked = jnp.concatenate([wide[:, :modes], stiff_diag[:, None], wide[:, modes + 1 :]], axis=1)
    together = jnp.concatenate([rhs, marked], axis=1)
    edges, inverse = pl.pallas_call(
        functools.partial(begin_kernel, nsub),
        out_shape=(
            jax.ShapeDtypeStruct((2, subs, together.shape[1], slot), f32),
            jax.ShapeDtypeStruct((4,) + coarse_inverse.shape, f32),
        ),
        in_specs=[vmem, vmem],
        out_specs=(vmem, vmem),
        scratch_shapes=[dma((2,)), dma((2,)), dma((3,)), dma((3,)), dma],
        compiler_params=pltpu.CompilerParams(
            collective_id=2, has_side_effects=True, vmem_limit_bytes=16 * 1024 * 1024
        ),
        name="begin",
    )(together[:, :, : 2 * slot], coarse_inverse)
    pieces = [edges[0], edges[1]]
    for colour in range(2, 6):
        window = together[:, :, colour * slot : (colour + 1) * slot]
        pieces.append(jnp.concatenate([window[t : t + 1] for t in lookup[colour - 2]], axis=0))
    across = jnp.concatenate(pieces, axis=-1)
    mask = usable[:, None, :]
    residual = mask * (rhs - across[:, :loads])
    precond = mask * (stiff_diag[:, None] + across[:, loads + modes : loads + modes + 1])

    own = subs * modes
    order = nsub * own
    inverse = jnp.pad(inverse.reshape(order, order), ((own, own), (0, 0)))
    near = lax.dynamic_slice_in_dim(inverse, sub_index * own, 3 * own, axis=0)
    before, mine, after = near[:own], near[own : 2 * own], near[2 * own :]
    near = jnp.concatenate(
        [mine, jnp.where(even, after, before), jnp.where(even, before, after)], axis=0
    )
    widen = np.zeros((order, nsub * subs * 8), np.float32)
    for at in range(order):
        widen[at, at // modes * 8 + at % modes] = 1.0
    choose = np.zeros((subs, 8, 8, 3, subs, modes), np.float32)
    for s in range(subs):
        sources = [(0, s), (1, s), (2, s)] + [(0, int(lookup[c][s])) for c in range(4)]
        for j, (group, t) in enumerate(sources):
            for m in range(modes):
                choose[s, j, m, group, t, m] = 1.0
    choose = choose.reshape(subs * 64, 3 * own)
    solver = jnp.dot(near, jnp.asarray(widen), precision=PRECISE)
    solver = jnp.dot(jnp.asarray(choose), solver, precision=PRECISE)

    other = jnp.pad(-mask * across[:, loads : loads + modes], ((0, 0), (0, 8 - modes), (0, 0)))
    slots = jnp.asarray(np.repeat(np.eye(6, dtype=np.float32), slot, axis=1))
    spread = (other[:, None] * slots[None, :, None, :]).reshape(subs, 48, interface)
    basis = jnp.concatenate([wide * mask, spread, jnp.zeros((subs, 8, interface), f32)], axis=1)

    vector = jax.ShapeDtypeStruct((subs, loads, interface), f32)
    small = jax.ShapeDtypeStruct((loads, 128), f32)

    def operate(search):
        return pl.pallas_call(
            functools.partial(operate_kernel, nsub, lookup),
            out_shape=(vector, small),
            in_specs=[anywhere, vmem, vmem],
            out_specs=(vmem, vmem),
            scratch_shapes=[
                pltpu.VMEM((subs, rows, interface), f32),
                pltpu.VMEM((subs, 4, loads, interface), f32),
                pltpu.VMEM((subs, 4, loads, rows), f32),
                pltpu.VMEM((subs, loads, interface), f32),
                pltpu.VMEM((2, subs, loads, slot), f32),
                dma((subs,)),
                dma((3, subs)),
                dma((3, subs)),
                dma((3, subs)),
                dma((3, subs)),
                dma((subs,)),
                dma((2,)),
                dma((2,)),
            ],
            compiler_params=pltpu.CompilerParams(
                collective_id=0, has_side_effects=True, vmem_limit_bytes=48 * 1024 * 1024
            ),
            name="operate",
        )(schur_block, search, mask)

    def lift(v, extra):
        out, total = pl.pallas_call(
            functools.partial(project_kernel, nsub),
            out_shape=(vector, small),
            in_specs=[vmem] * 5,
            out_specs=(vmem, vmem),
            scratch_shapes=[
                pltpu.VMEM((loads, 128), f32),
                pltpu.VMEM((nsub, loads, 128), f32),
                dma((nsub,)),
                dma((nsub,)),
            ],
            compiler_params=pltpu.CompilerParams(
                collective_id=1, has_side_effects=True, vmem_limit_bytes=32 * 1024 * 1024
            ),
            name="lift",
        )(v, extra, wide, solver, basis)
        return out, total[:, 64:65]

    def dots(a, b):
        return jnp.broadcast_to(jnp.sum(a * b, axis=(0, 2))[:, None], (loads, 128))

    lifted, _ = lift(residual, jnp.zeros((loads, 128), f32))
    projected = residual - lifted
    scaled = precond * projected
    lifted, energy = lift(scaled, 0.5 * dots(projected, scaled))
    search = scaled - lifted
    multipliers = None
    for iteration in range(ITERS):
        image, curve = operate(search)
        lifted, curve = lift(image, curve)
        step = energy / curve
        moved = step[None] * search
        multipliers = moved if multipliers is None else multipliers + moved
        projected = projected - step[None] * (image - lifted)
        if iteration + 1 < ITERS:
            scaled = precond * projected
            lifted, energy_new = lift(scaled, 0.5 * dots(projected, scaled))
            search = scaled - lifted + (energy_new / energy)[None] * search
            energy = energy_new
    return (jnp.swapaxes(multipliers, 0, 1), jnp.swapaxes(projected, 0, 1))


def shards(schur_block, rigid_modes, coarse_inverse, dual_rhs, stiff_diag, face_length):
    fits = dual_rhs.shape[0] == 8 and lax.axis_size("crs") == 4 and lax.axis_size("sub") <= 8
    build = by_kernels if fits else by_collectives
    return build(schur_block, rigid_modes, coarse_inverse, dual_rhs, stiff_diag, face_length)


def solution(mesh):
    return jax.shard_map(
        shards,
        mesh=mesh,
        in_specs=(
            P("sub", "crs", None),
            P("sub", None, None),
            P("crs", None),
            P("crs", "sub", None),
            P("sub", None),
            P("sub", None),
        ),
        out_specs=(P("crs", "sub", None), P("crs", "sub", None)),
        check_vma=False,
    )
```

```python
import functools

import jax
import jax.numpy as jnp
import numpy as np
from jax import lax
from jax.experimental import pallas as pl
from jax.experimental.pallas import tpu as pltpu
from jax.sharding import PartitionSpec as P

ITERS = 2
SY = 2
SZ = 4
SUBS = 8

PRECISE = lax.Precision.HIGHEST
SPLIT = lax.Precision.HIGH


def local_lookup():
    indices = np.arange(SUBS)
    coords = [indices // SZ, indices % SZ]
    extent = [SY, SZ]
    stride = [SZ, 1]
    lookup = np.zeros((4, SUBS), np.int32)
    for colour in range(4):
        axis_pick = colour // 2
        anchor = coords[axis_pick]
        offset = np.where(anchor % 2 == colour % 2, 1, -1)
        target = anchor + offset
        inside = (target >= 0) & (target < extent[axis_pick])
        lookup[colour] = np.where(inside, indices + offset * stride[axis_pick], indices)
    return lookup


def by_collectives(schur_block, rigid_modes, coarse_inverse, dual_rhs, stiff_diag, face_length):
    loads, subs, interface = dual_rhs.shape
    slot = interface // 6
    modes = rigid_modes.shape[1]
    own = subs * modes
    nsub = lax.axis_size("sub")
    sub_index = lax.axis_index("sub")
    even = sub_index % 2 == 0
    lookup = local_lookup()
    positions = jnp.arange(interface) % slot
    usable = (jnp.repeat(face_length, slot, axis=1) > positions[None, :]).astype(jnp.float32)
    up = [(i, i + 1) for i in range(nsub - 1)]
    down = [(i + 1, i) for i in range(nsub - 1)]

    def partner(vector):
        first = vector[..., :slot]
        second = vector[..., slot : 2 * slot]
        from_left = lax.ppermute(jnp.where(even, first, second), "sub", up)
        from_right = lax.ppermute(jnp.where(even, second, first), "sub", down)
        pieces = [jnp.where(even, from_right, from_left), jnp.where(even, from_left, from_right)]
        for colour in range(2, 6):
            window = vector[..., colour * slot : (colour + 1) * slot]
            pieces.append(
                jnp.concatenate([window[..., t : t + 1, :] for t in lookup[colour - 2]], axis=-2)
            )
        return jnp.concatenate(pieces, axis=-1)

    modes_first = jnp.swapaxes(rigid_modes, 0, 1)
    together = jnp.concatenate([dual_rhs, modes_first, stiff_diag[None]], axis=0)
    across = partner(together)
    residual = usable * (dual_rhs - across[:loads])
    modes_across = across[loads : loads + modes]
    precond = usable * (stiff_diag + across[-1])

    inverse = lax.all_gather(coarse_inverse, "crs", axis=0, tiled=True)

    def by_slot(array):
        return array.reshape(array.shape[:-1] + (6, slot))

    basis = by_slot(usable * jnp.concatenate([modes_first, -modes_across], axis=0))

    weighted = by_slot(modes_first * precond)
    blocks = jnp.einsum("msck,nsck->scmn", weighted, basis, precision=PRECISE)
    total_subs = nsub * subs
    here = sub_index * subs + jnp.arange(subs)
    left = here - subs
    right = here + subs
    targets = [jnp.where(even, right, left), jnp.where(even, left, right)]
    for colour in range(2, 6):
        targets.append(sub_index * subs + jnp.asarray(lookup[colour - 2]))
    targets = jnp.stack(targets, axis=1)
    hot_across = (targets[:, :, None] == jnp.arange(total_subs)).astype(jnp.float32)
    hot_here = (here[:, None] == jnp.arange(total_subs)).astype(jnp.float32)
    dense = jnp.einsum("smn,st->smtn", blocks[..., :modes].sum(axis=1), hot_here, precision=PRECISE)
    dense = dense + jnp.einsum("scmn,sct->smtn", blocks[..., modes:], hot_across, precision=PRECISE)
    dense = dense.reshape(own, total_subs * modes)
    middle = lax.all_gather(dense, "sub", axis=0, tiled=True)

    def coarse(vector):
        return jnp.einsum("lsi,msi->lsm", vector, modes_first, precision=PRECISE).reshape(loads, own)

    def dots(a, b):
        return jnp.sum(a * b, axis=(1, 2))[:, None]

    def shared(parts):
        gathered = lax.all_gather(jnp.concatenate(parts, axis=1), "sub", axis=0)
        count = own * (sum(part.shape[1] == own for part in parts))
        outs = []
        for at in range(0, count, own):
            outs.append(jnp.swapaxes(gathered[:, :, at : at + own], 0, 1).reshape(loads, nsub * own))
        sums = jnp.sum(gathered[:, :, count:], axis=0)
        return outs, [sums[:, j : j + 1] for j in range(sums.shape[1])]

    def solve(values):
        return jnp.einsum("lb,ab->la", values, inverse, precision=PRECISE)

    def lifted(values):
        grid = values.reshape(loads, nsub, subs, modes)
        padded = jnp.pad(grid, ((0, 0), (1, 1), (0, 0), (0, 0)))
        near = lax.dynamic_slice_in_dim(padded, sub_index, 3, axis=1)
        before, mine, after = near[:, 0], near[:, 1], near[:, 2]
        pieces = [jnp.where(even, after, before), jnp.where(even, before, after)]
        for colour in range(2, 6):
            pieces.append(jnp.stack([mine[:, t] for t in lookup[colour - 2]], axis=1))
        other = jnp.stack(pieces, axis=2)
        mine = jnp.broadcast_to(mine[:, :, None], other.shape)
        factors = jnp.concatenate([mine, other], axis=-1)
        out = jnp.einsum("lscm,msck->lsck", factors, basis, precision=PRECISE)
        return out.reshape(loads, subs, interface)

    def direction(residual, c_res, c_scaled, power):
        y = solve(c_res)
        my = jnp.einsum("lb,ab->la", y, middle, precision=PRECISE)
        energy = 0.5 * power - 2.0 * jnp.sum(y * c_scaled, axis=1, keepdims=True)
        energy = energy + jnp.sum(y * my, axis=1, keepdims=True)
        t = solve(c_scaled - my)
        return precond * (residual - lifted(y)) - lifted(t), energy

    scaled = precond * residual
    (c_res, c_scaled), (power,) = shared([coarse(residual), coarse(scaled), dots(residual, scaled)])
    search, energy = direction(residual, c_res, c_scaled, power)
    multipliers = None
    for iteration in range(ITERS):
        by_rows = jnp.einsum(
            "sij,lsj->lsi",
            schur_block,
            lax.all_gather(search, "crs", axis=0, tiled=True),
            precision=SPLIT,
        )
        product = lax.all_to_all(by_rows, "crs", split_axis=0, concat_axis=2, tiled=True)
        image = usable * (product - partner(product))
        last = iteration + 1 == ITERS
        curve = dots(search, product)
        if last:
            (c_image,), (curve,) = shared([coarse(image), curve])
        else:
            scaled_image = precond * image
            parts = [
                coarse(image),
                coarse(scaled_image),
                curve,
                dots(residual, scaled_image),
                dots(image, scaled_image),
            ]
            (c_image, c_scaled_image), (curve, cross, square) = shared(parts)
        step = energy / curve
        moved = step[:, :, None] * search
        multipliers = moved if multipliers is None else multipliers + moved
        residual = residual - step[:, :, None] * image
        c_res = c_res - step * c_image
        if last:
            projected = residual - lifted(solve(c_res))
        else:
            c_scaled = c_scaled - step * c_scaled_image
            power = power - 2.0 * step * cross + step * step * square
            fresh, energy_new = direction(residual, c_res, c_scaled, power)
            search = fresh + (energy_new / energy)[:, :, None] * search
            energy = energy_new
    return (multipliers, projected)


MESH = pl.DeviceIdType.MESH


def across_rows(a, b, precision=None):
    return lax.dot_general(
        a, b, (((1,), (1,)), ((), ())), precision=precision, preferred_element_type=jnp.float32
    )


def halves(x):
    high = x.astype(jnp.bfloat16)
    return high, (x - high.astype(jnp.float32)).astype(jnp.bfloat16)


def load_copy(schur, hold, load_sem, s):
    return pltpu.make_async_copy(schur.at[s], hold.at[s], load_sem.at[s])


def operate(nsub, lookup, repeated, load, search, usable, image, hold, res, buffers):
    gath, product, across, gsend, grecv, asend, arecv, osem, fsend, frecv = buffers
    subs, loads, interface = search.shape
    rows = hold.shape[1]
    slot = interface // 6
    me = lax.axis_index("sub")
    q = lax.axis_index("crs")
    core = q % 2
    twin = q + 1 - 2 * core
    far = (q + 2) % 4
    diagonal = (twin + 2) % 4
    odd = me % 2
    first = me + 1 - 2 * odd
    second = me - 1 + 2 * odd
    has_second = jnp.logical_and(second >= 0, second < nsub)

    def remote(src, dst, send, recv, target):
        return pltpu.make_async_remote_copy(
            src_ref=src,
            dst_ref=dst,
            send_sem=send,
            recv_sem=recv,
            device_id=target,
            device_id_type=MESH,
        )

    def to_twin(s, block):
        return remote(search.at[s], gath.at[s, block], gsend.at[0, s], grecv.at[0, s], (me, twin))

    def to_far(s, block):
        return remote(search.at[s], gath.at[s, block], gsend.at[1, s], grecv.at[1, s], (me, far))

    def relay(s, source, block):
        return remote(
            gath.at[s, source], gath.at[s, block], gsend.at[2, s], grecv.at[2, s], (me, twin)
        )

    def spread(s, carry):
        to_far(s, q).start()
        to_twin(s, q).start()
        return carry

    lax.fori_loop(0, subs, spread, 0)
    gath[:, q] = search[...]

    def forward(s):
        to_far(s, far).wait_recv()
        relay(s, far, far).start()

    peers = (twin, far, diagonal)
    own_columns = pl.ds(pl.multiple_of(q * rows, 128), rows)

    def give(s, j):
        return remote(
            res.at[s, peers[j]],
            product.at[s, :, own_columns],
            asend.at[j, s],
            arecv.at[j, s],
            (me, peers[j]),
        )

    def taken(s, j):
        columns = pl.ds(pl.multiple_of(peers[j] * rows, 128), rows)
        return remote(
            res.at[s, peers[j]],
            product.at[s, :, columns],
            asend.at[j, s],
            arecv.at[j, s],
            (me, peers[j]),
        )

    def keep(s):
        return pltpu.make_async_copy(res.at[s, q], product.at[s, :, own_columns], osem.at[s])

    forward(0)

    def multiply(s, carry):
        @pl.when(s + 1 < subs)
        def _():
            forward(s + 1)

        if not repeated:
            load(s).wait()
        w_high, w_low = halves(hold[s])
        to_twin(s, twin).wait_recv()
        relay(s, far, diagonal).wait_recv()
        x_high, x_low = halves(gath[s].reshape(4 * loads, interface))
        both = across_rows(jnp.concatenate([x_high, x_low], axis=0), w_high)
        out = both[: 4 * loads] + both[4 * loads :] + across_rows(x_high, w_low)
        res[s] = out.reshape(4, loads, rows)
        for j in range(3):
            give(s, j).start()
        keep(s).start()
        return carry

    lax.fori_loop(0, subs, multiply, 0)

    def finish(s, carry):
        keep(s).wait()
        for j in range(3):
            taken(s, j).wait_recv()
        return carry

    lax.fori_loop(0, subs, finish, 0)

    def face(c, target):
        return remote(
            product.at[:, :, pl.ds(c * slot, slot)],
            across.at[c],
            fsend.at[c],
            frecv.at[c],
            (target, q),
        )

    face(0, first).start()

    @pl.when(has_second)
    def _():
        face(1, second).start()

    @pl.when(jnp.logical_not(has_second))
    def _():
        across[1] = jnp.zeros(across.shape[1:], jnp.float32)

    total = jnp.zeros((loads, interface), jnp.float32)
    for s in range(subs):
        total = total + search[s] * product[s]
        for c in range(2, 6):
            at = pl.ds(c * slot, slot)
            other = int(lookup[c - 2][s])
            image[s, :, at] = usable[s, :, at] * (product[s, :, at] - product[other, :, at])
    curve = jnp.sum(total, axis=1, keepdims=True)

    def drain(s, carry):
        to_twin(s, q).wait_send()
        to_far(s, q).wait_send()
        relay(s, far, far).wait_send()
        for j in range(3):
            give(s, j).wait_send()
        return carry

    lax.fori_loop(0, subs, drain, 0)
    face(0, first).wait()

    @pl.when(has_second)
    def _():
        face(1, second).wait()

    for c in range(2):
        at = pl.ds(c * slot, slot)
        for s in range(subs):
            image[s, :, at] = usable[s, :, at] * (product[s, :, at] - across[c, s])
    return curve


def lift(nsub, v, extra, modes, solver, basis, lifted, msg, buffers):
    gat, send, recv = buffers
    subs, loads, _ = v.shape
    me = lax.axis_index("sub")
    q = lax.axis_index("crs")
    msg[...] = jnp.broadcast_to(extra, msg.shape)
    for s in range(subs):
        msg[:, 8 * s : 8 * s + 8] = across_rows(v[s], modes[s], PRECISE)

    def copy(k, block):
        return pltpu.make_async_remote_copy(
            src_ref=msg,
            dst_ref=gat.at[block],
            send_sem=send.at[k],
            recv_sem=recv.at[k],
            device_id=((me + k) % nsub, q),
            device_id_type=MESH,
        )

    for k in range(1, nsub):
        copy(k, me).start()
    gat[me] = msg[...]
    for k in range(1, nsub):
        copy(k, (me + nsub - k) % nsub).wait_recv()
    for k in range(1, nsub):
        copy(k, me).wait_send()
    pieces = [gat[t] for t in range(nsub)]
    total = functools.reduce(lambda a, b: a + b, pieces)
    values = jnp.concatenate([piece[:, : 8 * subs] for piece in pieces], axis=1)
    y = across_rows(values, solver[...], PRECISE)
    for s in range(subs):
        lifted[s] = jnp.dot(
            y[:, 64 * s : 64 * s + 64],
            basis[s],
            precision=PRECISE,
            preferred_element_type=jnp.float32,
        )
    return total[:, 64:65]


def main_kernel(
    nsub,
    lookup,
    schur,
    residual,
    precond,
    usable,
    modes,
    solver,
    basis,
    multipliers,
    projected,
    hold,
    res,
    search,
    work,
    lifted,
    msg,
    load_sem,
    *buffers,
):
    subs, loads, interface = residual.shape
    me = lax.axis_index("sub")
    q = lax.axis_index("crs")
    load = functools.partial(load_copy, schur, hold, load_sem)

    def start_load(s, carry):
        load(s).start()
        return carry

    lax.fori_loop(0, subs, start_load, 0)
    barrier = pltpu.get_barrier_semaphore()
    for k in range(1, nsub):
        pl.semaphore_signal(
            barrier, inc=1, device_id=((me + k) % nsub, q), device_id_type=MESH
        )
    for k in range(1, 4):
        pl.semaphore_signal(barrier, inc=1, device_id=(me, (q + k) % 4), device_id_type=MESH)
    pl.semaphore_wait(barrier, nsub + 2)

    operates = [buffers[10 * n : 10 * n + 10] for n in range(ITERS)]
    lifts = [buffers[10 * ITERS + 3 * n : 10 * ITERS + 3 * n + 3] for n in range(2 * ITERS + 1)]

    def lift_of(count, v, extra):
        return lift(nsub, v, extra, modes, solver, basis, lifted, msg, lifts[count])

    def scale():
        total = jnp.zeros((loads, interface), jnp.float32)
        for s in range(subs):
            scaled = precond[s] * projected[s]
            work[s] = scaled
            total = total + projected[s] * scaled
        return 0.5 * jnp.sum(total, axis=1, keepdims=True)

    lift_of(0, residual, jnp.zeros((loads, 1), jnp.float32))
    for s in range(subs):
        projected[s] = residual[s] - lifted[s]
    energy = lift_of(1, work, scale())
    for s in range(subs):
        search[s] = work[s] - lifted[s]
    for iteration in range(ITERS):
        curve = operate(
            nsub,
            lookup,
            iteration > 0,
            load,
            search,
            usable,
            work,
            hold,
            res,
            operates[iteration],
        )
        curve = lift_of(2 + 2 * iteration, work, curve)
        step = energy / curve
        for s in range(subs):
            moved = step * search[s]
            multipliers[s] = moved if iteration == 0 else multipliers[s] + moved
            projected[s] = projected[s] - step * (work[s] - lifted[s])
        if iteration + 1 < ITERS:
            energy_new = lift_of(3 + 2 * iteration, work, scale())
            ratio = energy_new / energy
            for s in range(subs):
                search[s] = work[s] - lifted[s] + ratio * search[s]
            energy = energy_new


def begin_kernel(nsub, edges, block, across, inverse, fsend, frecv, gsend, grecv, osem):
    me = lax.axis_index("sub")
    q = lax.axis_index("crs")
    core = q % 2
    twin = q + 1 - 2 * core
    far = (q + 2) % 4
    diagonal = (twin + 2) % 4
    odd = me % 2
    first = me + 1 - 2 * odd
    second = me - 1 + 2 * odd
    has_second = jnp.logical_and(second >= 0, second < nsub)
    slot = across.shape[3]
    barrier = pltpu.get_barrier_semaphore()
    for peer in (twin, far):
        pl.semaphore_signal(barrier, inc=1, device_id=(me, peer), device_id_type=MESH)
    pl.semaphore_signal(barrier, inc=1, device_id=(first, q), device_id_type=MESH)

    @pl.when(has_second)
    def _():
        pl.semaphore_signal(barrier, inc=1, device_id=(second, q), device_id_type=MESH)

    pl.semaphore_wait(barrier, jnp.where(has_second, 4, 3))

    def remote(src, dst, send, recv, target):
        return pltpu.make_async_remote_copy(
            src_ref=src,
            dst_ref=dst,
            send_sem=send,
            recv_sem=recv,
            device_id=target,
            device_id_type=MESH,
        )

    def to_far(at):
        return remote(block, inverse.at[at], gsend.at[1], grecv.at[1], (me, far))

    def to_twin(at):
        return remote(block, inverse.at[at], gsend.at[0], grecv.at[0], (me, twin))

    def relay(at):
        return remote(inverse.at[far], inverse.at[at], gsend.at[2], grecv.at[2], (me, twin))

    def face(c, target):
        return remote(
            edges.at[:, :, pl.ds(c * slot, slot)],
            across.at[c],
            fsend.at[c],
            frecv.at[c],
            (target, q),
        )

    keep = pltpu.make_async_copy(block, inverse.at[q], osem)
    to_far(q).start()
    to_twin(q).start()
    face(0, first).start()

    @pl.when(has_second)
    def _():
        face(1, second).start()

    keep.start()

    @pl.when(jnp.logical_not(has_second))
    def _():
        across[1] = jnp.zeros(across.shape[1:], jnp.float32)

    to_far(far).wait_recv()
    relay(far).start()
    keep.wait()
    to_twin(twin).wait_recv()
    to_far(q).wait_send()
    to_twin(q).wait_send()
    face(0, first).wait()

    @pl.when(has_second)
    def _():
        face(1, second).wait()

    relay(diagonal).wait_recv()
    relay(far).wait_send()


def by_kernels(schur_block, rigid_modes, coarse_inverse, dual_rhs, stiff_diag, face_length):
    loads, subs, interface = dual_rhs.shape
    rows = schur_block.shape[1]
    slot = interface // 6
    modes = rigid_modes.shape[1]
    nsub = lax.axis_size("sub")
    sub_index = lax.axis_index("sub")
    even = sub_index % 2 == 0
    lookup = local_lookup()
    positions = jnp.arange(interface) % slot
    usable = (jnp.repeat(face_length, slot, axis=1) > positions[None, :]).astype(jnp.float32)
    f32 = jnp.float32

    vmem = pl.BlockSpec(memory_space=pltpu.VMEM)
    anywhere = pl.BlockSpec(memory_space=pl.ANY)
    dma = pltpu.SemaphoreType.DMA

    rhs = jnp.swapaxes(dual_rhs, 0, 1)
    wide = jnp.pad(rigid_modes, ((0, 0), (0, 8 - modes), (0, 0)))
    marked = jnp.concatenate([wide[:, :modes], stiff_diag[:, None], wide[:, modes + 1 :]], axis=1)
    together = jnp.concatenate([rhs, marked], axis=1)
    edges, inverse = pl.pallas_call(
        functools.partial(begin_kernel, nsub),
        out_shape=(
            jax.ShapeDtypeStruct((2, subs, together.shape[1], slot), f32),
            jax.ShapeDtypeStruct((4,) + coarse_inverse.shape, f32),
        ),
        in_specs=[vmem, vmem],
        out_specs=(vmem, vmem),
        scratch_shapes=[dma((2,)), dma((2,)), dma((3,)), dma((3,)), dma],
        compiler_params=pltpu.CompilerParams(
            collective_id=1, has_side_effects=True, vmem_limit_bytes=16 * 1024 * 1024
        ),
        name="begin",
    )(together[:, :, : 2 * slot], coarse_inverse)
    pieces = [edges[0], edges[1]]
    for colour in range(2, 6):
        window = together[:, :, colour * slot : (colour + 1) * slot]
        pieces.append(jnp.concatenate([window[t : t + 1] for t in lookup[colour - 2]], axis=0))
    across = jnp.concatenate(pieces, axis=-1)
    mask = usable[:, None, :]
    residual = mask * (rhs - across[:, :loads])
    precond = mask * (stiff_diag[:, None] + across[:, loads + modes : loads + modes + 1])

    own = subs * modes
    order = nsub * own
    inverse = jnp.pad(inverse.reshape(order, order), ((own, own), (0, 0)))
    near = lax.dynamic_slice_in_dim(inverse, sub_index * own, 3 * own, axis=0)
    before, mine, after = near[:own], near[own : 2 * own], near[2 * own :]
    near = jnp.concatenate(
        [mine, jnp.where(even, after, before), jnp.where(even, before, after)], axis=0
    )
    widen = np.zeros((order, nsub * subs * 8), np.float32)
    for at in range(order):
        widen[at, at // modes * 8 + at % modes] = 1.0
    choose = np.zeros((subs, 8, 8, 3, subs, modes), np.float32)
    for s in range(subs):
        sources = [(0, s), (1, s), (2, s)] + [(0, int(lookup[c][s])) for c in range(4)]
        for j, (group, t) in enumerate(sources):
            for m in range(modes):
                choose[s, j, m, group, t, m] = 1.0
    choose = choose.reshape(subs * 64, 3 * own)
    solver = jnp.dot(near, jnp.asarray(widen), precision=PRECISE)
    solver = jnp.dot(jnp.asarray(choose), solver, precision=PRECISE)

    other = jnp.pad(-mask * across[:, loads : loads + modes], ((0, 0), (0, 8 - modes), (0, 0)))
    slots = jnp.asarray(np.repeat(np.eye(6, dtype=np.float32), slot, axis=1))
    spread = (other[:, None] * slots[None, :, None, :]).reshape(subs, 48, interface)
    basis = jnp.concatenate([wide * mask, spread, jnp.zeros((subs, 8, interface), f32)], axis=1)

    vector = jax.ShapeDtypeStruct((subs, loads, interface), f32)

    each_operate = [
        pltpu.VMEM((subs, 4, loads, interface), f32),
        pltpu.VMEM((subs, loads, interface), f32),
        pltpu.VMEM((2, subs, loads, slot), f32),
        dma((3, subs)),
        dma((3, subs)),
        dma((3, subs)),
        dma((3, subs)),
        dma((subs,)),
        dma((2,)),
        dma((2,)),
    ]
    each_lift = [pltpu.VMEM((nsub, loads, 128), f32), dma((nsub,)), dma((nsub,))]
    held = pltpu.VMEM((subs, loads, interface), f32)
    multipliers, projected = pl.pallas_call(
        functools.partial(main_kernel, nsub, lookup),
        out_shape=(vector, vector),
        in_specs=[anywhere] + [vmem] * 6,
        out_specs=(vmem, vmem),
        scratch_shapes=[
            pltpu.VMEM((subs, rows, interface), f32),
            pltpu.VMEM((subs, 4, loads, rows), f32),
            held,
            held,
            held,
            pltpu.VMEM((loads, 128), f32),
            dma((subs,)),
        ]
        + each_operate * ITERS
        + each_lift * (2 * ITERS + 1),
        compiler_params=pltpu.CompilerParams(
            collective_id=0, has_side_effects=True, vmem_limit_bytes=48 * 1024 * 1024
        ),
        name="main",
    )(schur_block, residual, precond, mask, wide, solver, basis)
    return (jnp.swapaxes(multipliers, 0, 1), jnp.swapaxes(projected, 0, 1))


def shards(schur_block, rigid_modes, coarse_inverse, dual_rhs, stiff_diag, face_length):
    fits = dual_rhs.shape[0] == 8 and lax.axis_size("crs") == 4 and lax.axis_size("sub") <= 8
    build = by_kernels if fits else by_collectives
    return build(schur_block, rigid_modes, coarse_inverse, dual_rhs, stiff_diag, face_length)


def solution(mesh):
    return jax.shard_map(
        shards,
        mesh=mesh,
        in_specs=(
            P("sub", "crs", None),
            P("sub", None, None),
            P("crs", None),
            P("crs", "sub", None),
            P("sub", None),
            P("sub", None),
        ),
        out_specs=(P("crs", "sub", None), P("crs", "sub", None)),
        check_vma=False,
    )
```
